32 devices in a mesh: dp: 4 (over y, core), fsdp: 8 (over z, x).
Axes of the slice: x: 2, y: 2, z: 4, core: 2. Of those that a mesh axis runs over, the one named last changes fastest.
Arguments:
- tokens: bfloat16 [16384, 768], P(('dp', 'fsdp')), may hold values from -6 to 6
- cotangent: bfloat16 [16384, 768], P(('dp', 'fsdp')), may hold values from -6 to 6
- send_row: int32 [32, 512], P(('dp', 'fsdp')), may hold values from 0 to 511, each once within a row
- seq_len: int32 [32, 4], P(('dp', 'fsdp')), may hold values from 0 to 512, as said below
- joint_weight: bfloat16 [768, 2304], P(('dp', 'fsdp')), may hold values from -0.3125 to 0.3125
- joint_bias: bfloat16 [1536], P(('dp', 'fsdp')), may hold values from -3 to 3
- output_weight: bfloat16 [768, 768], P(('dp', 'fsdp')), may hold values from -0.625 to 0.625
- output_bias: bfloat16 [768], P(('dp', 'fsdp')), may hold values from -2 to 2
- first_gain: bfloat16 [768], P(('dp', 'fsdp')), may hold values from 0.5 to 1.5
- first_shift: bfloat16 [768], P(('dp', 'fsdp')), may hold values from -2 to 2
- up_weight: bfloat16 [768, 3072], P(('dp', 'fsdp')), may hold values from -0.21875 to 0.21875
- up_bias: bfloat16 [3072], P(('dp', 'fsdp')), may hold values from -3 to 3
- down_weight: bfloat16 [3072, 768], P(('dp', 'fsdp')), may hold values from -0.15625 to 0.15625
- down_bias: bfloat16 [768], P(('dp', 'fsdp')), may hold values from -2 to 2
- second_gain: bfloat16 [768], P(('dp', 'fsdp')), may hold values from 0.5 to 1.5
- second_shift: bfloat16 [768], P(('dp', 'fsdp')), may hold values from -2 to 2
Outputs:
- layer_out: bfloat16 [16384, 768], P(('dp', 'fsdp'))
- grad_tokens: bfloat16 [16384, 768], P(('dp', 'fsdp'))
- grad_joint_weight: float32 [768, 2304], P(('dp', 'fsdp'))
- grad_joint_bias: float32 [1536], P(('dp', 'fsdp'))
- grad_output_weight: float32 [768, 768], P(('dp', 'fsdp'))
- grad_output_bias: float32 [768], P(('dp', 'fsdp'))
- grad_first_gain: float32 [768], P(('dp', 'fsdp'))
- grad_first_shift: float32 [768], P(('dp', 'fsdp'))
- grad_up_weight: float32 [768, 3072], P(('dp', 'fsdp'))
- grad_up_bias: float32 [3072], P(('dp', 'fsdp'))
- grad_down_weight: float32 [3072, 768], P(('dp', 'fsdp'))
- grad_down_bias: float32 [768], P(('dp', 'fsdp'))
- grad_second_gain: float32 [768], P(('dp', 'fsdp'))
- grad_second_shift: float32 [768], P(('dp', 'fsdp'))
The draws below stay inside these ranges and needn't reach their ends.
Inputs may be any that keep to these rules, and one draw needn't show every extreme that they name: `send_row`: each row is an ordering of the rows 0 to 511 of that device; send slot s of a device goes to the device s // 16 in dp+fsdp order. `seq_len`: a device's lengths sum to at most 512, the rest of its rows are padding; a length may be zero; some device holds a single sequence of 512 tokens.
All inputs are finite; a program needn't handle non-finite values.
Results may differ from the reference program's by a relative error of at most 0.015.
The reference program's roundings to bfloat16 on the way count: a program that leaves them out, or rounds other values in their place, can miss the bound.
Values may be sent and summed in bfloat16 or wider, within the bound.
A program may use at most 128 MiB of HBM per device.

```python
import jax
import jax.numpy as jnp
from jax import lax

D = 768
HD = 64
FF = 3072
TOK_DEV = 512
SEQ_DEV = 4
DEVS = 32
TOKENS = 16384


def draw_seq_len(key, part):
    key_total = jax.random.fold_in(key, 11)
    key_cut = jax.random.fold_in(key, 12)
    key_whole = jax.random.fold_in(key, 13)
    totals = jax.random.randint(key_total, (DEVS, 1), TOK_DEV // 2, TOK_DEV + 1)
    cuts = jax.random.randint(key_cut, (DEVS, SEQ_DEV - 1), 0, TOK_DEV + 1)
    cuts = jnp.sort(jnp.minimum(cuts, totals), axis=1)
    edges = jnp.concatenate([jnp.zeros((DEVS, 1), jnp.int32), cuts, totals], axis=1)
    lengths = edges[:, 1:] - edges[:, :-1]
    chosen = jax.random.randint(key_whole, (), 0, DEVS)
    single = jnp.concatenate([jnp.full((1,), TOK_DEV, jnp.int32), jnp.zeros((SEQ_DEV - 1,), jnp.int32)])
    picked = jnp.arange(DEVS)[:, None] == chosen
    return jnp.where(picked, single[None, :], lengths).astype(jnp.int32)


def level_of(key, shape, shards, least, top_value):
    level = 1.0
    for axis_at, shards_of in shards:
        heights = jax.random.uniform(jax.random.fold_in(jax.random.fold_in(key, 6), axis_at), (shards_of,), jnp.float32, least / len(shards), top_value / len(shards))
        level = level * jnp.repeat(jnp.exp(heights), shape[axis_at] // shards_of).reshape((-1,) + (1,) * (len(shape) - 1 - axis_at))
    return level


def normal_values(key, dims, scale, limit, pieces=(), held_as=jnp.bfloat16):
    factor_of = level_of(key, dims, pieces, -0.22, 0.18) if pieces else 1.0
    drawn = jax.random.normal(key, dims, jnp.float32) * scale * factor_of
    return jnp.minimum(jnp.maximum(drawn, -limit), limit).astype(held_as)


def setup_inputs(seed: int = 0) -> dict:
    key_of = jax.random.split(jax.random.key(seed), 17)
    return {
        "tokens": normal_values(key_of[0], (TOKENS, D), 1.0, 6.0, ((0, 32),)),
        "cotangent": normal_values(key_of[1], (TOKENS, D), 1.0, 6.0, ((0, 32),)),
        "send_row": jax.vmap(lambda own: jax.random.permutation(own, TOK_DEV))(jax.random.split(key_of[2], DEVS)).reshape((DEVS, TOK_DEV)).astype(jnp.int32),
        "seq_len": draw_seq_len(jax.random.fold_in(key_of[16], 71), 0),
        "joint_weight": normal_values(key_of[4], (D, 3 * D), (D // 2) ** -0.5, 0.3125, ((0, 32),)),
        "joint_bias": normal_values(key_of[5], (2 * D,), 0.5, 3.0, ((0, 32),)),
        "output_weight": normal_values(key_of[6], (D, D), (D // 8) ** -0.5, 0.625, ((0, 32),)),
        "output_bias": normal_values(key_of[7], (D,), 0.3, 2.0, ((0, 32),)),
        "first_gain": jnp.clip(1.0 + 0.1 * jax.random.normal(key_of[8], (D,), jnp.float32), 0.5, 1.5).astype(jnp.bfloat16),
        "first_shift": normal_values(key_of[9], (D,), 0.3, 2.0, ((0, 32),)),
        "up_weight": normal_values(key_of[10], (D, FF), D ** -0.5, 0.21875, ((0, 32),)),
        "up_bias": normal_values(key_of[11], (FF,), 0.5, 3.0, ((0, 32),)),
        "down_weight": normal_values(key_of[12], (FF, D), (FF // 2) ** -0.5, 0.15625, ((0, 32),)),
        "down_bias": normal_values(key_of[13], (D,), 0.3, 2.0, ((0, 32),)),
        "second_gain": jnp.clip(1.0 + 0.1 * jax.random.normal(key_of[14], (D,), jnp.float32), 0.5, 1.5).astype(jnp.bfloat16),
        "second_shift": normal_values(key_of[15], (D,), 0.3, 2.0, ((0, 32),)),
    }


@jax.custom_vjp
def low(v):
    return lax.optimization_barrier(v.astype(jnp.bfloat16)).astype(jnp.float32)

@jax.custom_vjp
def low_back(v):
    return v

def low_keep(v):
    return (low(v), None)

def low_pass(kept, grad):
    return (grad,)

def back_keep(v):
    return (v, None)

def back_low(kept, grad):
    return (low(grad),)
low.defvjp(low_keep, low_pass)
low_back.defvjp(back_keep, back_low)
norm_epsilon = 1e-12
masked_score = -1e+30

def matmul_high(left, right):
    return jnp.dot(left, right, precision=lax.Precision.HIGHEST)

def layer_norm(value, norm_gain, norm_shift):
    row_mean = lax.optimization_barrier(jnp.mean(value, axis=-1, keepdims=True))
    centered = value - row_mean
    variance = lax.optimization_barrier(jnp.mean(centered * centered, axis=-1, keepdims=True))
    return centered * lax.rsqrt(variance + norm_epsilon) * norm_gain + norm_shift

def forward(inputs, params, segment):
    joint_weight, joint_bias, output_weight, output_bias, first_gain, first_shift, up_weight, up_bias, down_weight, down_bias, second_gain, second_shift = params
    row_count = inputs.shape[0]
    model_width = inputs.shape[1]
    head_count = model_width // HD
    score_scale = HD ** (-0.5)
    bias_joint = jnp.concatenate([joint_bias[:model_width], jnp.zeros((model_width,), jnp.float32), joint_bias[model_width:]])
    joint = low_back(low(matmul_high(inputs, joint_weight) + bias_joint))
    query_heads = joint[:, :model_width].reshape(row_count, head_count, HD)
    key_heads = joint[:, model_width:2 * model_width].reshape(row_count, head_count, HD)
    value_heads = joint[:, 2 * model_width:].reshape(row_count, head_count, HD)
    scores = low_back(jnp.einsum('qhd,khd->hqk', query_heads, key_heads, precision=lax.Precision.HIGHEST) * score_scale)
    same_segment = segment[:, None] == segment[None, :]
    scores = jnp.where(same_segment[None], scores, masked_score)
    attn_probs = low(jax.nn.softmax(scores, axis=-1))
    attended = jnp.einsum('hqk,khd->qhd', attn_probs, value_heads, precision=lax.Precision.HIGHEST)
    attended = low_back(low(attended.reshape(row_count, model_width)))
    branch = low_back(matmul_high(attended, output_weight) + output_bias)
    first_norm = layer_norm(inputs + branch, first_gain, first_shift)
    hidden = low_back(matmul_high(low(first_norm), up_weight) + up_bias)
    active = low(jax.nn.gelu(hidden, approximate=False))
    second = low_back(matmul_high(active, down_weight) + down_bias)
    return layer_norm(first_norm + second, second_gain, second_shift)

def reference(tokens, cotangent, send_row, seq_len, joint_weight, joint_bias, output_weight, output_bias, first_gain, first_shift, up_weight, up_bias, down_weight, down_bias, second_gain, second_shift):
    device_count = send_row.shape[0]
    row_count = send_row.shape[1]
    model_width = tokens.shape[1]
    piece_rows = row_count // device_count
    source = send_row.reshape(device_count, device_count, piece_rows).astype(jnp.int32)
    row_base = (jnp.arange(device_count, dtype=jnp.int32) * row_count)[:, None, None]
    dealt_index = jnp.transpose(source + row_base, (1, 0, 2)).reshape(device_count, row_count).astype(jnp.int32)
    seq_ends = jnp.cumsum(seq_len, axis=1).astype(jnp.int32)
    position = jnp.arange(row_count, dtype=jnp.int32)
    segment = lax.optimization_barrier(jnp.sum((position[None, :, None] >= seq_ends[:, None, :]).astype(jnp.int32), axis=2)).astype(jnp.int32)
    valid_rows = (segment < seq_len.shape[1]).astype(jnp.float32)
    params = [weight_arg.astype(jnp.float32) for weight_arg in (joint_weight, joint_bias, output_weight, output_bias, first_gain, first_shift, up_weight, up_bias, down_weight, down_bias, second_gain, second_shift)]

    def per_device(running, device_item):
        take_rows, seg_rows, keep_rows = device_item
        inputs = tokens[take_rows].astype(jnp.float32)
        upstream = cotangent[take_rows].astype(jnp.float32) * keep_rows[:, None]

        def layer_call(layer_in, layer_params):
            return forward(layer_in, layer_params, seg_rows)
        result, pullback = jax.vjp(layer_call, inputs, params)
        grad_inputs, grad_params = pullback(upstream)
        running = [summed_grad + device_grad for summed_grad, device_grad in zip(running, grad_params)]
        return (running, (result.astype(jnp.bfloat16), grad_inputs.astype(jnp.bfloat16)))
    start_sums = [jnp.zeros_like(weight_arg) for weight_arg in params]
    weight_sums, (dealt_out, dealt_grads) = lax.scan(per_device, start_sums, (dealt_index, segment, valid_rows))
    flat_index = dealt_index.reshape(-1)
    layer_out = jnp.zeros_like(tokens).at[flat_index].set(dealt_out.reshape(-1, model_width))
    grad_tokens = jnp.zeros_like(tokens).at[flat_index].set(dealt_grads.reshape(-1, model_width))
    return (layer_out, grad_tokens, weight_sums[0], weight_sums[1], weight_sums[2], weight_sums[3], weight_sums[4], weight_sums[5], weight_sums[6], weight_sums[7], weight_sums[8], weight_sums[9], weight_sums[10], weight_sums[11])
```

```python
import jax
import jax.numpy as jnp
from jax import lax
from jax.experimental import pallas as pl
from jax.experimental.pallas import tpu as pltpu
from jax.sharding import PartitionSpec as P

HD = 64


norm_epsilon = 1e-12
masked_score = -1e30


def transpose_dot(left, right):
    return lax.dot_general(
        left, right, (((0,), (0,)), ((), ())), preferred_element_type=jnp.float32
    )


def dot_right_t(left, right):
    return lax.dot_general(
        left, right, (((1,), (1,)), ((), ())), preferred_element_type=jnp.float32
    )


def normalize(value):
    row_mean = jnp.mean(value, axis=-1, keepdims=True)
    centered = value - row_mean
    variance = jnp.mean(centered * centered, axis=-1, keepdims=True)
    inverse = lax.rsqrt(variance + norm_epsilon)
    return (centered * inverse, inverse)


def normalize_back(upstream, normed, inverse, norm_gain):
    scaled = upstream * norm_gain
    grad_value = inverse * (
        scaled
        - jnp.mean(scaled, axis=-1, keepdims=True)
        - normed * jnp.mean(scaled * normed, axis=-1, keepdims=True)
    )
    return (grad_value, jnp.sum(upstream * normed, axis=0), jnp.sum(upstream, axis=0))


def exact_gelu(value):
    return jax.nn.gelu(value, approximate=False)


def plain_body(
    tokens,
    cotangent,
    send_row,
    seq_len,
    joint_weight,
    joint_bias,
    output_weight,
    output_bias,
    first_gain,
    first_shift,
    up_weight,
    up_bias,
    down_weight,
    down_bias,
    second_gain,
    second_shift,
):
    slot_rows = send_row[0]
    row_count = slot_rows.shape[0]
    model_width = tokens.shape[1]
    head_count = model_width // HD
    score_scale = HD ** (-0.5)
    block_rows = min(512, row_count)
    dealt, upstream = (
        lax.all_to_all(tokens[slot_rows], ("dp", "fsdp"), split_axis=0, concat_axis=0, tiled=True),
        lax.all_to_all(
            cotangent[slot_rows], ("dp", "fsdp"), split_axis=0, concat_axis=0, tiled=True
        ),
    )
    shards = (
        joint_weight,
        joint_bias,
        output_weight,
        output_bias,
        first_gain,
        first_shift,
        up_weight,
        up_bias,
        down_weight,
        down_bias,
        second_gain,
        second_shift,
    )
    gathered = (
        lax.all_gather(shards[0], ("dp", "fsdp"), axis=0, tiled=True),
        lax.all_gather(shards[1], ("dp", "fsdp"), axis=0, tiled=True),
        lax.all_gather(shards[2], ("dp", "fsdp"), axis=0, tiled=True),
        lax.all_gather(shards[3], ("dp", "fsdp"), axis=0, tiled=True),
        lax.all_gather(shards[4], ("dp", "fsdp"), axis=0, tiled=True),
        lax.all_gather(shards[5], ("dp", "fsdp"), axis=0, tiled=True),
        lax.all_gather(shards[6], ("dp", "fsdp"), axis=0, tiled=True),
        lax.all_gather(shards[7], ("dp", "fsdp"), axis=0, tiled=True),
        lax.all_gather(shards[8], ("dp", "fsdp"), axis=0, tiled=True),
        lax.all_gather(shards[9], ("dp", "fsdp"), axis=0, tiled=True),
        lax.all_gather(shards[10], ("dp", "fsdp"), axis=0, tiled=True),
        lax.all_gather(shards[11], ("dp", "fsdp"), axis=0, tiled=True),
    )
    (
        joint_all,
        joint_bias_all,
        output_all,
        output_bias_all,
        first_gain_all,
        first_shift_all,
        up_all,
        up_bias_all,
        down_all,
        down_bias_all,
        second_gain_all,
        second_shift_all,
    ) = gathered
    seq_ends = jnp.cumsum(seq_len[0])
    position = jnp.arange(row_count, dtype=jnp.int32)
    segment = jnp.sum((position[:, None] >= seq_ends[None, :]).astype(jnp.int32), axis=1)
    valid_rows = (segment < seq_len.shape[1]).astype(jnp.float32)
    bias_wide = joint_bias_all.astype(jnp.float32)
    bias_joint = jnp.concatenate(
        [bias_wide[:model_width], jnp.zeros((model_width,), jnp.float32), bias_wide[model_width:]]
    )
    joint_low = (jnp.dot(dealt, joint_all, preferred_element_type=jnp.float32) + bias_joint).astype(
        jnp.bfloat16
    )
    query_heads = joint_low[:, :model_width].reshape(row_count, head_count, HD)
    key_heads = joint_low[:, model_width : 2 * model_width].reshape(row_count, head_count, HD)
    value_heads = joint_low[:, 2 * model_width :].reshape(row_count, head_count, HD)

    def block_scores(block_start):
        scores = (
            jnp.einsum("qhd,khd->hqk", query_heads, key_heads, preferred_element_type=jnp.float32)
            * score_scale
        )
        same_segment = segment[block_start : block_start + block_rows, None] == segment[None, :]
        return (jnp.where(same_segment[None], scores, masked_score), query_heads)

    block_start = 0
    scores, query_block = block_scores(block_start)
    row_peak = jnp.max(scores, axis=-1, keepdims=True)
    exponent = jnp.exp(scores - row_peak)
    row_total = jnp.sum(exponent, axis=-1, keepdims=True)
    probs_low = (exponent / row_total).astype(jnp.bfloat16)
    attended_parts = jnp.einsum(
        "hqk,khd->qhd", probs_low, value_heads, preferred_element_type=jnp.float32
    )
    log_totals = [row_peak + jnp.log(row_total)]
    attended_low = attended_parts.reshape(row_count, model_width).astype(jnp.bfloat16)
    branch = jnp.dot(
        attended_low, output_all, preferred_element_type=jnp.float32
    ) + output_bias_all.astype(jnp.float32)
    normed_one, inverse_one = normalize(dealt.astype(jnp.float32) + branch)
    first_norm = normed_one * first_gain_all.astype(jnp.float32) + first_shift_all.astype(
        jnp.float32
    )
    first_low = first_norm.astype(jnp.bfloat16)
    hidden = jnp.dot(first_low, up_all, preferred_element_type=jnp.float32) + up_bias_all.astype(
        jnp.float32
    )
    active_low = exact_gelu(hidden).astype(jnp.bfloat16)
    second = jnp.dot(
        active_low, down_all, preferred_element_type=jnp.float32
    ) + down_bias_all.astype(jnp.float32)
    normed_two, inverse_two = normalize(first_norm + second)
    dealt_out = (
        normed_two * second_gain_all.astype(jnp.float32) + second_shift_all.astype(jnp.float32)
    ).astype(jnp.bfloat16)
    out_home = lax.all_to_all(dealt_out, ("dp", "fsdp"), split_axis=0, concat_axis=0, tiled=True)
    gathered = (
        lax.all_gather(shards[0], ("dp", "fsdp"), axis=0, tiled=True),
        lax.all_gather(shards[1], ("dp", "fsdp"), axis=0, tiled=True),
        lax.all_gather(shards[2], ("dp", "fsdp"), axis=0, tiled=True),
        lax.all_gather(shards[3], ("dp", "fsdp"), axis=0, tiled=True),
        lax.all_gather(shards[4], ("dp", "fsdp"), axis=0, tiled=True),
        lax.all_gather(shards[5], ("dp", "fsdp"), axis=0, tiled=True),
        lax.all_gather(shards[6], ("dp", "fsdp"), axis=0, tiled=True),
        lax.all_gather(shards[7], ("dp", "fsdp"), axis=0, tiled=True),
        lax.all_gather(shards[8], ("dp", "fsdp"), axis=0, tiled=True),
        lax.all_gather(shards[9], ("dp", "fsdp"), axis=0, tiled=True),
        lax.all_gather(shards[10], ("dp", "fsdp"), axis=0, tiled=True),
        lax.all_gather(shards[11], ("dp", "fsdp"), axis=0, tiled=True),
    )
    (
        joint_all,
        joint_bias_all,
        output_all,
        output_bias_all,
        first_gain_all,
        first_shift_all,
        up_all,
        up_bias_all,
        down_all,
        down_bias_all,
        second_gain_all,
        second_shift_all,
    ) = gathered
    grad_top = upstream.astype(jnp.float32) * valid_rows[:, None]
    grad_second, grad_second_gain, grad_second_shift = normalize_back(
        grad_top, normed_two, inverse_two, second_gain_all.astype(jnp.float32)
    )
    grad_second_low = grad_second.astype(jnp.bfloat16)
    grad_down_weight = transpose_dot(active_low, grad_second_low)
    grad_down_bias = jnp.sum(grad_second_low.astype(jnp.float32), axis=0)
    grad_active = dot_right_t(grad_second_low, down_all)
    gelu_pull = jax.vjp(exact_gelu, hidden)[1]
    grad_hidden_low = gelu_pull(grad_active)[0].astype(jnp.bfloat16)
    grad_up_weight = transpose_dot(first_low, grad_hidden_low)
    grad_up_bias = jnp.sum(grad_hidden_low.astype(jnp.float32), axis=0)
    grad_first = grad_second + dot_right_t(grad_hidden_low, up_all)
    grad_summed, grad_first_gain, grad_first_shift = normalize_back(
        grad_first, normed_one, inverse_one, first_gain_all.astype(jnp.float32)
    )
    grad_branch_low = grad_summed.astype(jnp.bfloat16)
    grad_output_weight = transpose_dot(attended_low, grad_branch_low)
    grad_output_bias = jnp.sum(grad_branch_low.astype(jnp.float32), axis=0)
    grad_attended = (
        dot_right_t(grad_branch_low, output_all)
        .astype(jnp.bfloat16)
        .reshape(row_count, head_count, HD)
    )
    grad_key = jnp.zeros((row_count, head_count, HD), jnp.float32)
    grad_value = jnp.zeros((row_count, head_count, HD), jnp.float32)
    grad_query_parts = []
    for block_number, block_start in enumerate(range(0, row_count, block_rows)):
        scores, query_block = block_scores(block_start)
        attn_probs = jnp.exp(scores - log_totals[block_number])
        probs_low = attn_probs.astype(jnp.bfloat16)
        grad_value = jnp.einsum(
            "hqk,qhd->khd", probs_low, grad_attended, preferred_element_type=jnp.float32
        )
        grad_probs = jnp.einsum(
            "qhd,khd->hqk", grad_attended, value_heads, preferred_element_type=jnp.float32
        )
        grad_scores = (
            attn_probs * (grad_probs - jnp.sum(attn_probs * grad_probs, axis=-1, keepdims=True))
        ).astype(jnp.bfloat16)
        grad_query_parts.append(
            jnp.einsum("hqk,khd->qhd", grad_scores, key_heads, preferred_element_type=jnp.float32)
            * score_scale
        )
        grad_key = (
            jnp.einsum("hqk,qhd->khd", grad_scores, query_block, preferred_element_type=jnp.float32)
            * score_scale
        )
    grad_query = grad_query_parts[0]
    grad_joint_low = jnp.concatenate(
        [
            grad_query.reshape(row_count, model_width),
            grad_key.reshape(row_count, model_width),
            grad_value.reshape(row_count, model_width),
        ],
        axis=1,
    ).astype(jnp.bfloat16)
    grad_joint_weight = transpose_dot(dealt, grad_joint_low)
    joint_sums = jnp.sum(grad_joint_low.astype(jnp.float32), axis=0)
    grad_joint_bias = jnp.concatenate([joint_sums[:model_width], joint_sums[2 * model_width :]])
    grad_dealt_low = (grad_summed + dot_right_t(grad_joint_low, joint_all)).astype(jnp.bfloat16)
    owned = (
        lax.psum_scatter(grad_joint_weight, ("dp", "fsdp"), scatter_dimension=0, tiled=True),
        lax.psum_scatter(grad_joint_bias, ("dp", "fsdp"), scatter_dimension=0, tiled=True),
        lax.psum_scatter(grad_output_weight, ("dp", "fsdp"), scatter_dimension=0, tiled=True),
        lax.psum_scatter(grad_output_bias, ("dp", "fsdp"), scatter_dimension=0, tiled=True),
        lax.psum_scatter(grad_first_gain, ("dp", "fsdp"), scatter_dimension=0, tiled=True),
        lax.psum_scatter(grad_first_shift, ("dp", "fsdp"), scatter_dimension=0, tiled=True),
        lax.psum_scatter(grad_up_weight, ("dp", "fsdp"), scatter_dimension=0, tiled=True),
        lax.psum_scatter(grad_up_bias, ("dp", "fsdp"), scatter_dimension=0, tiled=True),
        lax.psum_scatter(grad_down_weight, ("dp", "fsdp"), scatter_dimension=0, tiled=True),
        lax.psum_scatter(grad_down_bias, ("dp", "fsdp"), scatter_dimension=0, tiled=True),
        lax.psum_scatter(grad_second_gain, ("dp", "fsdp"), scatter_dimension=0, tiled=True),
        lax.psum_scatter(grad_second_shift, ("dp", "fsdp"), scatter_dimension=0, tiled=True),
    )
    grad_home = lax.all_to_all(
        grad_dealt_low, ("dp", "fsdp"), split_axis=0, concat_axis=0, tiled=True
    )
    layer_out = jnp.zeros_like(tokens).at[slot_rows].set(out_home)
    grad_tokens = jnp.zeros_like(tokens).at[slot_rows].set(grad_home)
    return (layer_out, grad_tokens) + tuple(owned)


MESH_ID = pl.DeviceIdType.MESH
PARTS_Y, PARTS_C, PARTS_Z, PARTS_X = 2, 2, 4, 2
VEC_WIDTH = 384


def fits_fast(mesh):
    return mesh.shape["dp"] == 4 and mesh.shape["fsdp"] == 8


def place():
    dp = lax.axis_index("dp")
    fsdp = lax.axis_index("fsdp")
    return dp // 2, dp % 2, fsdp // 2, fsdp % 2


def device_of(y, c, z, x):
    return (y * 2 + c, z * 2 + x)


def greet_all():
    barrier = pltpu.get_barrier_semaphore()
    me = lax.axis_index("dp") * 8 + lax.axis_index("fsdp")

    def greet(step, carry):
        other = lax.rem(me + step, 32)
        pl.semaphore_signal(
            barrier, inc=1, device_id=(other // 8, other % 8), device_id_type=MESH_ID
        )
        return carry

    lax.fori_loop(1, 32, greet, 0)
    pl.semaphore_wait(barrier, 31)


def remote(src, dst, send_sem, recv_sem, device):
    return pltpu.make_async_remote_copy(
        src_ref=src,
        dst_ref=dst,
        send_sem=send_sem,
        recv_sem=recv_sem,
        device_id=device,
        device_id_type=MESH_ID,
    )


def exchange_start(src, dst, send_sem, recv_sem, local_sem):
    me = lax.axis_index("dp") * 8 + lax.axis_index("fsdp")

    def send(step, carry):
        other = lax.rem(me + step, 32)
        remote(src.at[other], dst.at[me], send_sem, recv_sem, (other // 8, other % 8)).start()
        return carry

    pltpu.make_async_copy(src.at[me], dst.at[me], local_sem).start()
    lax.fori_loop(1, 32, send, 0)


def exchange_wait(src, dst, send_sem, recv_sem, local_sem):
    me = lax.axis_index("dp") * 8 + lax.axis_index("fsdp")
    device = (lax.axis_index("dp"), lax.rem(lax.axis_index("fsdp") + 1, 8))
    pltpu.make_async_copy(src.at[me], dst.at[me], local_sem).wait()
    whole = remote(src.at[pl.ds(0, 31)], dst.at[pl.ds(0, 31)], send_sem, recv_sem, device)
    whole.wait_send()
    whole.wait_recv()


GATHER_CHUNKS = (
    (0, 0, 2304),
    (1, 0, 768),
    (2, 0, 1536),
    (2, 1536, 1536),
    (3, 0, 384),
    (3, 384, 384),
)


def gather_kernel(
    tok_in, cot_in, vec_in, wj, wo, wu, wd,
    tok_out, cot_out, vec_out, aj, ao, au, ad,
    ex_send, ex_recv, ex_local, own_sem, z_send, z_recv, f_send, f_recv, d_send, d_recv,
):
    y, c, z, x = place()
    shards = (wj, wo, wu, wd)
    whole = (aj, ao, au, ad)
    count = len(GATHER_CHUNKS)
    own = [
        pltpu.make_async_copy(shards[w], whole[w].at[y, c, z, x], own_sem.at[w]) for w in range(4)
    ]
    for copy in own:
        copy.start()
    greet_all()
    exchange_start(tok_in, tok_out, ex_send.at[0], ex_recv.at[0], ex_local.at[0])

    def at(chunk, *index):
        w, first, width = GATHER_CHUNKS[chunk]
        return whole[w].at[(*index, slice(None), pl.ds(first, width))]

    def z_copy(chunk, k):
        w, first, width = GATHER_CHUNKS[chunk]
        return remote(
            shards[w].at[:, pl.ds(first, width)],
            at(chunk, y, c, z, x),
            z_send.at[chunk, k - 1],
            z_recv.at[chunk, k - 1],
            device_of(y, c, lax.rem(z + k, 4), x),
        )

    first_peer = device_of(jnp.where(c == 0, y, 1 - y), c, z, jnp.where(c == 0, 1 - x, x))
    second_peer = device_of(jnp.where(c == 0, 1 - y, y), c, z, jnp.where(c == 0, x, 1 - x))
    sibling = device_of(y, 1 - c, z, x)
    y_first, x_first = jnp.where(c == 0, y, 1 - y), jnp.where(c == 0, 1 - x, x)

    def first_copy(chunk):
        ref = at(chunk, y, c, slice(None), x)
        return remote(ref, ref, f_send.at[chunk, 0], f_recv.at[chunk, 0], first_peer)

    def second_copy(chunk, core):
        ref = at(chunk, y, c, slice(None), slice(None)) if core == 0 else at(chunk, slice(None), c, slice(None), x)
        return remote(ref, ref, f_send.at[chunk, 1], f_recv.at[chunk, 1], second_peer)

    def by_core(act):
        for core in range(2):
            pl.when(c == core)(lambda core=core: act(core))

    def sibling_copy(chunk, part, core):
        if part == 0:
            ref = at(chunk, y, c, slice(None), x)
        elif part == 1:
            ref = at(chunk, y_first, c, slice(None), x_first)
        elif core == 0:
            ref = at(chunk, 1 - y, c, slice(None), slice(None))
        else:
            ref = at(chunk, slice(None), c, slice(None), 1 - x)
        return remote(ref, ref, d_send.at[chunk, part], d_recv.at[chunk, part], sibling)

    for chunk in range(count):
        for k in (1, 2, 3):
            z_copy(chunk, k).start()
    exchange_start(vec_in, vec_out, ex_send.at[2], ex_recv.at[2], ex_local.at[2])
    exchange_start(cot_in, cot_out, ex_send.at[1], ex_recv.at[1], ex_local.at[1])
    for copy in own:
        copy.wait()
    for tick in range(count + 2):
        chunk = tick
        if chunk < count:
            for k in (1, 2, 3):
                z_copy(chunk, k).wait_recv()
            first_copy(chunk).start()
            sibling_copy(chunk, 0, 0).start()
        chunk = tick - 1
        if 0 <= chunk < count:
            first_copy(chunk).wait_recv()
            by_core(lambda core: second_copy(chunk, core).start())
            sibling_copy(chunk, 1, 0).start()
        chunk = tick - 2
        if 0 <= chunk < count:
            by_core(lambda core: second_copy(chunk, core).wait_recv())
            by_core(lambda core: sibling_copy(chunk, 2, core).start())
    for chunk in range(count):
        for k in (1, 2, 3):
            z_copy(chunk, k).wait_send()
        first_copy(chunk).wait_send()
        by_core(lambda core: second_copy(chunk, core).wait_send())
        for part in range(2):
            sibling_copy(chunk, part, 0).wait()
        by_core(lambda core: sibling_copy(chunk, 2, core).wait())
    exchange_wait(tok_in, tok_out, ex_send.at[0], ex_recv.at[0], ex_local.at[0])
    exchange_wait(vec_in, vec_out, ex_send.at[2], ex_recv.at[2], ex_local.at[2])
    exchange_wait(cot_in, cot_out, ex_send.at[1], ex_recv.at[1], ex_local.at[1])


def gather_all(tok, cot, vec, shards):
    count = len(GATHER_CHUNKS)
    hbm = pl.BlockSpec(memory_space=pltpu.HBM)
    dma = pltpu.SemaphoreType.DMA
    outs = pl.pallas_call(
        gather_kernel,
        out_shape=[
            jax.ShapeDtypeStruct(tok.shape, tok.dtype),
            jax.ShapeDtypeStruct(cot.shape, cot.dtype),
            jax.ShapeDtypeStruct(vec.shape, vec.dtype),
        ]
        + [
            jax.ShapeDtypeStruct((PARTS_Y, PARTS_C, PARTS_Z, PARTS_X) + s.shape, s.dtype)
            for s in shards
        ],
        in_specs=[hbm] * 7,
        out_specs=[hbm] * 7,
        scratch_shapes=[
            dma((3,)), dma((3,)), dma((3,)), dma((4,)),
            dma((count, 3)), dma((count, 3)), dma((count, 2)), dma((count, 2)),
            dma((count, 3)), dma((count, 3)),
        ],
        compiler_params=pltpu.CompilerParams(collective_id=0, has_side_effects=True),
        name="gather_all",
    )(tok, cot, vec, *shards)
    tok_all, cot_all, vec_all, *weights = outs
    weights = [w.reshape(-1, w.shape[-1]) for w in weights]
    return tok_all.reshape(-1, tok.shape[-1]), cot_all.reshape(-1, cot.shape[-1]), vec_all, weights


SCATTER_CHUNKS = (
    (0, 0, 384),
    (0, 384, 384),
    (1, 0, 1536),
    (1, 1536, 1536),
    (2, 0, 768),
    (3, 0, 1152),
    (3, 1152, 1152),
)
SCATTER_ROWS = (96, 24, 24, 24)


def scatter_kernel(
    out_in, grad_in, vec_in, gd, gu, go, gj,
    out_home, grad_home, vec_home, sd, su, so, sj,
    *scratch,
):
    count = len(SCATTER_CHUNKS)
    mine = scratch[0:count]
    from_core = scratch[count : 2 * count]
    from_first = scratch[2 * count : 3 * count]
    from_second = scratch[3 * count : 4 * count]
    from_z = scratch[4 * count : 5 * count]
    (vec_got, ex_send, ex_recv, ex_local, load_sem, d_send, d_recv, f_send, f_recv, z_send, z_recv) = scratch[
        5 * count :
    ]
    grads = (gd, gu, go, gj)
    sums = (sd, su, so, sj)
    y, c, z, x = place()
    sibling = device_of(y, 1 - c, z, x)
    first_peer = device_of(jnp.where(c == 0, 1 - y, y), c, z, jnp.where(c == 0, x, 1 - x))
    second_peer = device_of(jnp.where(c == 0, y, 1 - y), c, z, jnp.where(c == 0, 1 - x, x))
    p_own, q_own = jnp.where(c == 0, y, x), jnp.where(c == 0, x, y)

    def source(chunk, core, yy, xx):
        g, first, width = SCATTER_CHUNKS[chunk]
        return grads[g].at[yy, core, :, xx, :, pl.ds(first, width)]

    def load(chunk, p, q):
        yy, xx = jnp.where(c == 0, p, q), jnp.where(c == 0, q, p)
        return pltpu.make_async_copy(
            source(chunk, c, yy, xx), mine[chunk].at[p, q], load_sem.at[chunk, 2 * p + q]
        )

    def core_copy(chunk, p, q):
        yy, xx = jnp.where(c == 1, p, q), jnp.where(c == 1, q, p)
        return remote(
            source(chunk, 1 - c, yy, xx),
            from_core[chunk].at[p, q],
            d_send.at[chunk, 2 * p + q],
            d_recv.at[chunk, 2 * p + q],
            sibling,
        )

    def first_copy(chunk):
        return remote(
            mine[chunk].at[1 - p_own], from_first[chunk], f_send.at[chunk, 0], f_recv.at[chunk, 0], first_peer
        )

    def second_copy(chunk):
        return remote(
            mine[chunk].at[p_own, 1 - q_own],
            from_second[chunk],
            f_send.at[chunk, 1],
            f_recv.at[chunk, 1],
            second_peer,
        )

    def z_copy(chunk, k):
        return remote(
            mine[chunk].at[p_own, q_own, lax.rem(z + k, 4)],
            from_z[chunk].at[k - 1],
            z_send.at[chunk, k - 1],
            z_recv.at[chunk, k - 1],
            device_of(y, c, lax.rem(z + k, 4), x),
        )

    greet_all()
    exchange_start(out_in, out_home, ex_send.at[0], ex_recv.at[0], ex_local.at[0])
    exchange_start(vec_in, vec_got, ex_send.at[2], ex_recv.at[2], ex_local.at[2])
    quads = [(p, q) for p in range(2) for q in range(2)]
    for chunk in range(count):
        for p, q in quads:
            core_copy(chunk, p, q).start()
            load(chunk, p, q).start()
    exchange_start(grad_in, grad_home, ex_send.at[1], ex_recv.at[1], ex_local.at[1])

    def wide(ref):
        return ref[...].astype(jnp.float32)

    for tick in range(count + 3):
        chunk = tick
        if chunk < count:
            for p, q in quads:
                core_copy(chunk, p, q).wait_recv()
                load(chunk, p, q).wait()

            def add_first(i, carry):
                q, zz = i // 4, lax.rem(i, 4)
                ref = mine[chunk].at[1 - p_own, q, zz]
                ref[...] = (wide(ref) + wide(from_core[chunk].at[1 - p_own, q, zz])).astype(jnp.bfloat16)
                return carry

            lax.fori_loop(0, 8, add_first, 0)
            first_copy(chunk).start()
        chunk = tick - 1
        if 0 <= chunk < count:
            first_copy(chunk).wait_recv()

            def add_second(zz, carry):
                ref = mine[chunk].at[p_own, 1 - q_own, zz]
                ref[...] = (
                    wide(ref)
                    + wide(from_core[chunk].at[p_own, 1 - q_own, zz])
                    + wide(from_first[chunk].at[1 - q_own, zz])
                ).astype(jnp.bfloat16)
                return carry

            lax.fori_loop(0, 4, add_second, 0)
            second_copy(chunk).start()
        chunk = tick - 2
        if 0 <= chunk < count:
            second_copy(chunk).wait_recv()

            def add_z(k, carry):
                zz = lax.rem(z + k, 4)
                ref = mine[chunk].at[p_own, q_own, zz]
                ref[...] = (
                    wide(ref)
                    + wide(from_core[chunk].at[p_own, q_own, zz])
                    + wide(from_first[chunk].at[q_own, zz])
                    + wide(from_second[chunk].at[zz])
                ).astype(jnp.bfloat16)
                return carry

            lax.fori_loop(1, 4, add_z, 0)
            for k in (1, 2, 3):
                z_copy(chunk, k).start()
        chunk = tick - 3
        if 0 <= chunk < count:
            for k in (1, 2, 3):
                z_copy(chunk, k).wait_recv()
            g, first, width = SCATTER_CHUNKS[chunk]
            sums[g][:, pl.ds(first, width)] = (
                wide(mine[chunk].at[p_own, q_own, z])
                + wide(from_core[chunk].at[p_own, q_own, z])
                + wide(from_first[chunk].at[q_own, z])
                + wide(from_second[chunk].at[z])
                + wide(from_z[chunk].at[0])
                + wide(from_z[chunk].at[1])
                + wide(from_z[chunk].at[2])
            )
    exchange_wait(vec_in, vec_got, ex_send.at[2], ex_recv.at[2], ex_local.at[2])
    vec_home[...] = jnp.sum(vec_got[...], axis=0)
    for chunk in range(count):
        for p, q in quads:
            core_copy(chunk, p, q).wait_send()
        first_copy(chunk).wait_send()
        second_copy(chunk).wait_send()
        for k in (1, 2, 3):
            z_copy(chunk, k).wait_send()
    exchange_wait(out_in, out_home, ex_send.at[0], ex_recv.at[0], ex_local.at[0])
    exchange_wait(grad_in, grad_home, ex_send.at[1], ex_recv.at[1], ex_local.at[1])


def scatter_all(out_low, grad_low, vec, grads):
    count = len(SCATTER_CHUNKS)
    hbm = pl.BlockSpec(memory_space=pltpu.HBM)
    vmem = pl.BlockSpec(memory_space=pltpu.VMEM)
    dma = pltpu.SemaphoreType.DMA
    shapes = [(SCATTER_ROWS[g], width) for g, _, width in SCATTER_CHUNKS]

    def held(*lead):
        return [pltpu.VMEM(lead + s, jnp.bfloat16) for s in shapes]

    parts = (PARTS_Y, PARTS_C, PARTS_Z, PARTS_X)
    rows = [g.reshape(parts + (g.shape[0] // 32, g.shape[1])) for g in grads]
    tok = (32, out_low.shape[0] // 32, out_low.shape[1])
    return pl.pallas_call(
        scatter_kernel,
        out_shape=[
            jax.ShapeDtypeStruct(tok, out_low.dtype),
            jax.ShapeDtypeStruct(tok, grad_low.dtype),
            jax.ShapeDtypeStruct(vec.shape[1:], jnp.float32),
        ]
        + [jax.ShapeDtypeStruct(r.shape[4:], jnp.float32) for r in rows],
        in_specs=[hbm] * 7,
        out_specs=[hbm, hbm] + [vmem] * 5,
        scratch_shapes=held(2, 2, 4)
        + held(2, 2, 4)
        + held(2, 4)
        + held(4)
        + held(3)
        + [
            pltpu.VMEM(vec.shape, jnp.float32),
            dma((3,)), dma((3,)), dma((3,)), dma((count, 4)), dma((count, 4)), dma((count, 4)),
            dma((count, 2)), dma((count, 2)), dma((count, 3)), dma((count, 3)),
        ],
        compiler_params=pltpu.CompilerParams(
            collective_id=1, has_side_effects=True, vmem_limit_bytes=48 << 20
        ),
        name="scatter_all",
    )(out_low.reshape(tok), grad_low.reshape(tok), vec, *rows)


def fast_body(
    tokens,
    cotangent,
    send_row,
    seq_len,
    joint_weight,
    joint_bias,
    output_weight,
    output_bias,
    first_gain,
    first_shift,
    up_weight,
    up_bias,
    down_weight,
    down_bias,
    second_gain,
    second_shift,
):
    slot_rows = send_row[0]
    row_count = slot_rows.shape[0]
    model_width = tokens.shape[1]
    head_count = model_width // HD
    score_scale = HD ** (-0.5)
    vectors = (
        joint_bias, output_bias, first_gain, first_shift, up_bias, down_bias, second_gain, second_shift,
    )
    widths = [v.shape[0] for v in vectors]
    packed = jnp.concatenate([v.astype(jnp.float32) for v in vectors])
    packed = jnp.pad(packed, (0, VEC_WIDTH - packed.shape[0]))
    packed = jnp.broadcast_to(packed.reshape(1, -1, 128), (32, VEC_WIDTH // 128, 128))
    dealt, upstream, vec_all, (joint_all, output_all, up_all, down_all) = gather_all(
        tokens[slot_rows].reshape(32, -1, model_width),
        cotangent[slot_rows].reshape(32, -1, model_width),
        packed,
        (joint_weight, output_weight, up_weight, down_weight),
    )
    vec_all = vec_all.reshape(32, VEC_WIDTH)
    starts = [sum(widths[:i]) for i in range(len(widths))]
    (
        joint_bias_all,
        output_bias_all,
        first_gain_all,
        first_shift_all,
        up_bias_all,
        down_bias_all,
        second_gain_all,
        second_shift_all,
    ) = [vec_all[:, s : s + w].reshape(-1) for s, w in zip(starts, widths)]
    seq_ends = jnp.cumsum(seq_len[0])
    position = jnp.arange(row_count, dtype=jnp.int32)
    segment = jnp.sum((position[:, None] >= seq_ends[None, :]).astype(jnp.int32), axis=1)
    valid_rows = (segment < seq_len.shape[1]).astype(jnp.float32)
    bias_wide = joint_bias_all
    bias_joint = jnp.concatenate(
        [bias_wide[:model_width], jnp.zeros((model_width,), jnp.float32), bias_wide[model_width:]]
    )
    joint_low = (jnp.dot(dealt, joint_all, preferred_element_type=jnp.float32) + bias_joint).astype(
        jnp.bfloat16
    )
    query_heads = joint_low[:, :model_width].reshape(row_count, head_count, HD)
    key_heads = joint_low[:, model_width : 2 * model_width].reshape(row_count, head_count, HD)
    value_heads = joint_low[:, 2 * model_width :].reshape(row_count, head_count, HD)
    scores = (
        jnp.einsum("qhd,khd->hqk", query_heads, key_heads, preferred_element_type=jnp.float32)
        * score_scale
    )
    same_segment = segment[:, None] == segment[None, :]
    scores = jnp.where(same_segment[None], scores, masked_score)
    row_peak = jnp.max(scores, axis=-1, keepdims=True)
    exponent = jnp.exp(scores - row_peak)
    row_total = jnp.sum(exponent, axis=-1, keepdims=True)
    probs_low = (exponent / row_total).astype(jnp.bfloat16)
    attended = jnp.einsum("hqk,khd->qhd", probs_low, value_heads, preferred_element_type=jnp.float32)
    log_total = row_peak + jnp.log(row_total)
    attended_low = attended.reshape(row_count, model_width).astype(jnp.bfloat16)
    branch = jnp.dot(attended_low, output_all, preferred_element_type=jnp.float32) + output_bias_all
    normed_one, inverse_one = normalize(dealt.astype(jnp.float32) + branch)
    first_norm = normed_one * first_gain_all + first_shift_all
    first_low = first_norm.astype(jnp.bfloat16)
    hidden = jnp.dot(first_low, up_all, preferred_element_type=jnp.float32) + up_bias_all
    active_low = exact_gelu(hidden).astype(jnp.bfloat16)
    second = jnp.dot(active_low, down_all, preferred_element_type=jnp.float32) + down_bias_all
    normed_two, inverse_two = normalize(first_norm + second)
    dealt_out = (normed_two * second_gain_all + second_shift_all).astype(jnp.bfloat16)
    grad_top = upstream.astype(jnp.float32) * valid_rows[:, None]
    grad_second, grad_second_gain, grad_second_shift = normalize_back(
        grad_top, normed_two, inverse_two, second_gain_all
    )
    grad_second_low = grad_second.astype(jnp.bfloat16)
    grad_down_weight = transpose_dot(active_low, grad_second_low)
    grad_down_bias = jnp.sum(grad_second_low.astype(jnp.float32), axis=0)
    grad_active = dot_right_t(grad_second_low, down_all)
    gelu_pull = jax.vjp(exact_gelu, hidden)[1]
    grad_hidden_low = gelu_pull(grad_active)[0].astype(jnp.bfloat16)
    grad_up_weight = transpose_dot(first_low, grad_hidden_low)
    grad_up_bias = jnp.sum(grad_hidden_low.astype(jnp.float32), axis=0)
    grad_first = grad_second + dot_right_t(grad_hidden_low, up_all)
    grad_summed, grad_first_gain, grad_first_shift = normalize_back(
        grad_first, normed_one, inverse_one, first_gain_all
    )
    grad_branch_low = grad_summed.astype(jnp.bfloat16)
    grad_output_weight = transpose_dot(attended_low, grad_branch_low)
    grad_output_bias = jnp.sum(grad_branch_low.astype(jnp.float32), axis=0)
    grad_attended = (
        dot_right_t(grad_branch_low, output_all)
        .astype(jnp.bfloat16)
        .reshape(row_count, head_count, HD)
    )
    attn_probs = jnp.exp(scores - log_total)
    probs_low = attn_probs.astype(jnp.bfloat16)
    grad_value = jnp.einsum(
        "hqk,qhd->khd", probs_low, grad_attended, preferred_element_type=jnp.float32
    )
    grad_probs = jnp.einsum(
        "qhd,khd->hqk", grad_attended, value_heads, preferred_element_type=jnp.float32
    )
    grad_scores = (
        attn_probs * (grad_probs - jnp.sum(attn_probs * grad_probs, axis=-1, keepdims=True))
    ).astype(jnp.bfloat16)
    grad_query = (
        jnp.einsum("hqk,khd->qhd", grad_scores, key_heads, preferred_element_type=jnp.float32)
        * score_scale
    )
    grad_key = (
        jnp.einsum("hqk,qhd->khd", grad_scores, query_heads, preferred_element_type=jnp.float32)
        * score_scale
    )
    grad_joint_low = jnp.concatenate(
        [
            grad_query.reshape(row_count, model_width),
            grad_key.reshape(row_count, model_width),
            grad_value.reshape(row_count, model_width),
        ],
        axis=1,
    ).astype(jnp.bfloat16)
    grad_joint_weight = transpose_dot(dealt, grad_joint_low)
    joint_sums = jnp.sum(grad_joint_low.astype(jnp.float32), axis=0)
    grad_joint_bias = jnp.concatenate([joint_sums[:model_width], joint_sums[2 * model_width :]])
    grad_dealt_low = (grad_summed + dot_right_t(grad_joint_low, joint_all)).astype(jnp.bfloat16)
    vector_grads = (
        grad_joint_bias, grad_output_bias, grad_first_gain, grad_first_shift,
        grad_up_bias, grad_down_bias, grad_second_gain, grad_second_shift,
    )
    packed = jnp.concatenate([v.reshape(32, -1) for v in vector_grads], axis=1)
    packed = jnp.pad(packed, ((0, 0), (0, VEC_WIDTH - packed.shape[1])))
    out_home, grad_home, vec_home, down_own, up_own, output_own, joint_own = scatter_all(
        dealt_out,
        grad_dealt_low,
        packed.reshape(32, VEC_WIDTH // 128, 128),
        [g.astype(jnp.bfloat16) for g in (grad_down_weight, grad_up_weight, grad_output_weight, grad_joint_weight)],
    )
    vec_home = vec_home.reshape(-1)
    own = [vec_home[s : s + w] for s, w in zip(starts, widths)]
    layer_out = jnp.zeros_like(tokens).at[slot_rows].set(out_home.reshape(row_count, model_width))
    grad_tokens = jnp.zeros_like(tokens).at[slot_rows].set(grad_home.reshape(row_count, model_width))
    return (
        layer_out, grad_tokens, joint_own, own[0], output_own, own[1], own[2], own[3],
        up_own, own[4], down_own, own[5], own[6], own[7],
    )


def solution(mesh):
    body = fast_body if fits_fast(mesh) else plain_body
    placed = (
        P(("dp", "fsdp"), None),
        P(("dp", "fsdp"), None),
        P(("dp", "fsdp"), None),
        P(("dp", "fsdp"), None),
        P(("dp", "fsdp"), None),
        P(("dp", "fsdp")),
        P(("dp", "fsdp"), None),
        P(("dp", "fsdp")),
        P(("dp", "fsdp")),
        P(("dp", "fsdp")),
        P(("dp", "fsdp"), None),
        P(("dp", "fsdp")),
        P(("dp", "fsdp"), None),
        P(("dp", "fsdp")),
        P(("dp", "fsdp")),
        P(("dp", "fsdp")),
    )
    return jax.shard_map(
        body,
        mesh=mesh,
        in_specs=placed,
        out_specs=(
            P(("dp", "fsdp"), None),
            P(("dp", "fsdp"), None),
            P(("dp", "fsdp"), None),
            P(("dp", "fsdp")),
            P(("dp", "fsdp"), None),
            P(("dp", "fsdp")),
            P(("dp", "fsdp")),
            P(("dp", "fsdp")),
            P(("dp", "fsdp"), None),
            P(("dp", "fsdp")),
            P(("dp", "fsdp"), None),
            P(("dp", "fsdp")),
            P(("dp", "fsdp")),
            P(("dp", "fsdp")),
        ),
        check_vma=False,
    )
```
